768 devices in a mesh: dom: 96 (over y, z), sub: 8 (over x, core).
Axes of the slice: x: 4, y: 8, z: 12, core: 2. Of those that a mesh axis runs over, the one named last changes fastest.
Arguments:
- coarse_state: float32 [9, 64, 98304], P(None, None, ('dom', 'sub')), may hold values from -6 to 6
- fine_nodal_state: float32 [9, 64, 98304], P(None, None, ('dom', 'sub')), may hold values from -6 to 6
- coarse_elastic: float32 [2, 98304], P(None, ('dom', 'sub')), may hold values from 1.2 to 4.8
- coarse_density: float32 [98304], P(('dom', 'sub')), may hold values from 0.5 to 1
- fine_lame_shear: float32 [2, 98304], P(None, ('dom', 'sub')), may hold values from 1.2 to 4.8
- fine_density: float32 [98304], P(('dom', 'sub')), may hold values from 0.5 to 1
- coarse_links: int32 [6, 98304], P(None, ('dom', 'sub')), may hold values from 0 to 383, as said below
- fine_links: int32 [6, 98304], P(None, ('dom', 'sub')), may hold values from 0 to 383, as said below
- coarse_send: int32 [98304], P(('dom', 'sub')), may hold values from 0 to 767, as said below
- fine_return: int32 [98304], P(('dom', 'sub')), may hold values from 0 to 767, as said below
- source_elem: int32 [3072], P(('dom', 'sub')), may hold values from 0 to 127
- source_amp: float32 [9, 3072], P(None, ('dom', 'sub')), may hold values from -6 to 6
- source_shape: float32 [64, 3072], P(None, ('dom', 'sub')), may hold values from -60 to 60
Outputs:
- coarse_final: float32 [9, 64, 98304], P(None, None, ('dom', 'sub'))
- fine_final: float32 [9, 64, 98304], P(None, None, ('dom', 'sub'))
The draws below stay inside these ranges and needn't reach their ends.
Inputs may be any that keep to these rules, and one draw needn't show every extreme that they name: `coarse_links`: entry (f, e) of a device's block names the element whose trace meets face f of local element e: local elements first, then 64 of the device below and 64 of the device above along dom+sub, then interface slot k at 256 + k. Slot k = b * 16 + s is read for slots b that device b returns. `fine_links`: as for coarse_links; slot k = a 16 + s holds what device a of the group sent. `coarse_send`: Face-major local face index for slot k = b * 16 + s toward sub index b; distinct within a device. `fine_return`: Face-major local face index for slot k = a 16 + s toward sub index a; distinct within a device.
All inputs are finite; a program needn't handle non-finite values.
Results may differ from the reference program's by a relative error of at most 0.0003.
Values sent between devices are 32-bit elements; how exact they have to be, the bound alone decides.
A program may use at most 64 MiB of HBM per device.

```python
import math
from functools import partial
import jax
import jax.numpy as jnp
import numpy as np
from jax import lax

VARS = 9
NODES = 64
ORDER = 4
ELEMS = 128
LAYERS = 2
LAYER = 64
SLOT = 16
IFACE = 128
SRC = 4
STEPS = 1
SUBSTEPS = 2
NDEV = 768
ETOT = 98304
SRC_ALL = 3072
N_SUB = 8


def layer_links(key):

    def one_device(device_key):
        key_list = jax.random.split(device_key, 4)

        def layer_permutation(layer_key):
            return jax.random.permutation(layer_key, LAYER)
        perm_x = jax.vmap(layer_permutation)(jax.random.split(key_list[0], LAYERS))
        perm_y = jax.vmap(layer_permutation)(jax.random.split(key_list[1], LAYERS))
        inverse_x = jnp.argsort(perm_x, axis=1)
        inverse_y = jnp.argsort(perm_y, axis=1)
        offsets = (jnp.arange(LAYERS) * LAYER)[:, None]
        lower_perm = jax.random.permutation(key_list[2], LAYER)
        upper_perm = jax.random.permutation(key_list[3], LAYER)
        element = jnp.arange(ELEMS)
        layer_of = element // LAYER
        within = element % LAYER
        z_lower = jnp.where(layer_of > 0, element - LAYER, ELEMS + lower_perm[within])
        z_upper = jnp.where(layer_of < LAYERS - 1, element + LAYER, ELEMS + LAYER + upper_perm[within])
        rows_all = [(inverse_x + offsets).reshape(-1), (perm_x + offsets).reshape(-1), (inverse_y + offsets).reshape(-1), (perm_y + offsets).reshape(-1), z_lower, z_upper]
        return jnp.stack(rows_all).astype(jnp.int32)
    return jax.vmap(one_device)(jax.random.split(key, NDEV))


def face_choice(key):
    total_faces = 6 * ELEMS

    def one_device(device_key):
        split_keys = jax.random.split(device_key)
        order_list = jax.random.permutation(split_keys[0], total_faces)
        spot_index = jax.random.randint(split_keys[1], (), 0, IFACE)
        where_top = jnp.argmax(order_list == total_faces - 1)
        order_list = order_list.at[where_top].set(order_list[spot_index]).at[spot_index].set(total_faces - 1)
        return order_list[:IFACE].astype(jnp.int32)
    return jax.vmap(one_device)(jax.random.split(key, NDEV))


def interface_plan(key):
    groups = NDEV // N_SUB
    key_list = jax.random.split(jax.random.fold_in(key, 7301), 5)
    counts = jax.random.randint(key_list[0], (groups, N_SUB, N_SUB), 1, SLOT + 1)
    full_receiver = jax.random.randint(key_list[1], (groups, 1, 1), 0, N_SUB)
    full_sender = jax.random.randint(key_list[2], (groups, 1, 1), 0, N_SUB)
    position = jnp.arange(N_SUB)
    counts = jnp.where(position[None, None, :] == full_receiver, SLOT, counts)
    counts = jnp.where(position[None, :, None] == full_sender, SLOT, counts)
    slot_index = jnp.arange(SLOT)
    live_sent = (slot_index[None, None, None, :] < counts[..., None]).reshape(NDEV, IFACE)
    live_taken = (slot_index[None, None, None, :] < jnp.transpose(counts, (0, 2, 1))[..., None]).reshape(NDEV, IFACE)
    return (live_sent, live_taken, face_choice(key_list[3]), face_choice(key_list[4]))


def linked(key, salt, live, faces):
    links = layer_links(jax.random.fold_in(key, salt))
    flat_links = links.reshape(NDEV, 6 * ELEMS)
    marks = ELEMS + 2 * LAYER + jnp.arange(IFACE)

    def override(row_links, face_list, live_list):
        return row_links.at[face_list].set(jnp.where(live_list, marks, row_links[face_list]))
    flat_links = jax.vmap(override)(flat_links, faces, live)
    return jnp.transpose(flat_links.reshape(NDEV, 6, ELEMS), (1, 0, 2)).reshape(6, NDEV * ELEMS).astype(jnp.int32)


def draw_coarse_links(key, part):
    live_sent, live_taken, coarse_faces, fine_faces = interface_plan(key)
    return linked(key, 11, live_sent, coarse_faces)


def draw_fine_links(key, part):
    live_sent, live_taken, coarse_faces, fine_faces = interface_plan(key)
    return linked(key, 13, live_taken, fine_faces)


def draw_coarse_send(key, part):
    return interface_plan(key)[2].reshape(-1)


def draw_fine_return(key, part):
    return interface_plan(key)[3].reshape(-1)


def with_ends(drawn, key, least, top_value):
    extent = drawn.shape
    spot = [jax.random.randint(jax.random.fold_in(key, axis), (), 0, extent[axis]) for axis in range(len(extent))]
    drawn = drawn.at[tuple(spot)].set(least)
    longest = extent.index(max(extent))
    spot[longest] = (spot[longest] + 1) % extent[longest]
    return drawn.at[tuple(spot)].set(top_value)


def block_levels(key, extent, cuts, low, largest):
    gain, own = 1.0, jax.random.fold_in(key, 6)
    for dim, blocks in cuts:
        draws = jnp.exp(jax.random.uniform(jax.random.fold_in(own, dim), (blocks,), jnp.float32, low / len(cuts), largest / len(cuts)))
        gain = gain * jnp.repeat(draws, extent[dim] // blocks).reshape([-1 if axis == dim else 1 for axis in range(len(extent))])
    return gain


def noise(key, shape, scale, bound, shards=(), held_as=jnp.bfloat16):
    entries = scale * jax.random.normal(key, shape, jnp.float32)
    if shards:
        entries = entries * block_levels(key, shape, shards, -0.22, 0.18)
    return jnp.clip(entries, -bound, bound).astype(held_as)


def setup_inputs(seed: int = 0) -> dict:
    streams_of = jax.random.split(jax.random.key(seed), 14)
    coarse_state = noise(streams_of[0], (VARS, NODES, ETOT), 1.0, 6.0, ((2, 768),), jnp.float32)
    fine_nodal_state = noise(streams_of[1], (VARS, NODES, ETOT), 1.0, 6.0, ((2, 768),), jnp.float32)
    coarse_elastic = jnp.clip(jnp.exp(math.log(4.8) - 1.3862944 * jax.random.uniform(streams_of[2], (2, ETOT), jnp.float32) ** block_levels(streams_of[2], (2, ETOT), ((1, 768),), -0.2, 0.2)), 1.2, 4.8)
    coarse_density = jnp.clip(jnp.exp(math.log(1.0) - 0.6931472 * jax.random.uniform(streams_of[3], (ETOT,), jnp.float32) ** block_levels(streams_of[3], (ETOT,), ((0, 768),), -0.2, 0.2)), 0.5, 1.0)
    fine_lame_shear = jnp.clip(jnp.exp(math.log(4.8) - 1.3862944 * jax.random.uniform(streams_of[4], (2, ETOT), jnp.float32) ** block_levels(streams_of[4], (2, ETOT), ((1, 768),), -0.2, 0.2)), 1.2, 4.8)
    fine_density = jnp.clip(jnp.exp(math.log(1.0) - 0.6931472 * jax.random.uniform(streams_of[5], (ETOT,), jnp.float32) ** block_levels(streams_of[5], (ETOT,), ((0, 768),), -0.2, 0.2)), 0.5, 1.0)
    coarse_links = draw_coarse_links(jax.random.fold_in(streams_of[13], 71), 0)
    fine_links = draw_fine_links(jax.random.fold_in(streams_of[13], 71), 0)
    coarse_send = draw_coarse_send(jax.random.fold_in(streams_of[13], 71), 0)
    fine_return = draw_fine_return(jax.random.fold_in(streams_of[13], 71), 0)
    source_elem = with_ends(jax.random.randint(streams_of[10], (SRC_ALL,), 0, ELEMS), jax.random.fold_in(streams_of[10], 1), 0, ELEMS - 1).astype(jnp.int32)
    source_amp = noise(streams_of[11], (VARS, SRC_ALL), 1.0, 6.0, ((1, 768),), jnp.float32)
    source_shape = noise(streams_of[12], (NODES, SRC_ALL), 10.0, 60.0, ((1, 768),), jnp.float32)
    return {"coarse_state": coarse_state, "fine_nodal_state": fine_nodal_state, "coarse_elastic": coarse_elastic, "coarse_density": coarse_density, "fine_lame_shear": fine_lame_shear, "fine_density": fine_density, "coarse_links": coarse_links, "fine_links": fine_links, "coarse_send": coarse_send, "fine_return": fine_return, "source_elem": source_elem, "source_amp": source_amp, "source_shape": source_shape}


highest_order = lax.Precision.HIGHEST
coarse_dt = 0.03
coarse_scale = 1.0
fine_scale = 2.0
lift_weight = 6.0

def derivative_tables():
    points = np.array([-1.0, -1.0 / math.sqrt(5.0), 1.0 / math.sqrt(5.0), 1.0])
    barycentric = np.array([1.0 / np.prod([points[col_index] - points[other_index] for other_index in range(4) if other_index != col_index]) for col_index in range(4)])
    derivative = np.zeros((4, 4))
    for row_index in range(4):
        for col_index in range(4):
            if row_index != col_index:
                derivative[row_index, col_index] = barycentric[col_index] / barycentric[row_index] / (points[row_index] - points[col_index])
        derivative[row_index, row_index] = -np.sum(derivative[row_index])
    eye_four = np.eye(4)
    along_x = np.kron(derivative, np.eye(16))
    along_y = np.kron(np.kron(eye_four, derivative), eye_four)
    along_z = np.kron(np.eye(16), derivative)
    return np.stack([along_x, along_y, along_z])

def make_material(elastic, density):
    lame = elastic[0]
    shear = elastic[1]
    buoyancy = 1.0 / density
    speed = jnp.sqrt((lame + 2.0 * shear) * buoyancy)
    return (lame, shear, buoyancy, speed)

def stress_rates(grad_x, grad_y, grad_z, material):
    lame, shear, buoyancy = (material[0], material[1], material[2])
    spread = grad_x[6] + grad_y[7] + grad_z[8]
    rates = [lame * spread + 2.0 * shear * grad_x[6], lame * spread + 2.0 * shear * grad_y[7], lame * spread + 2.0 * shear * grad_z[8], shear * (grad_y[6] + grad_x[7]), shear * (grad_z[7] + grad_y[8]), shear * (grad_z[6] + grad_x[8]), buoyancy * (grad_x[0] + grad_y[3] + grad_z[5]), buoyancy * (grad_x[3] + grad_y[1] + grad_z[4]), buoyancy * (grad_x[5] + grad_y[4] + grad_z[2])]
    return jnp.stack(rates)

def volume_rate(nodal_field, material, gradient_scale):
    lookup_tables = jnp.asarray(derivative_tables(), jnp.float32)
    spatial_gradients = jnp.einsum('ygq,kqp->ykgp', lookup_tables, nodal_field, precision=highest_order) * gradient_scale
    return stress_rates(spatial_gradients[0], spatial_gradients[1], spatial_gradients[2], material)

def face_traces(nodal_field):
    count_elems = nodal_field.shape[-1]
    cube = nodal_field.reshape(9, 4, 4, 4, count_elems)
    slices = [cube[:, 0], cube[:, 3], cube[:, :, 0], cube[:, :, 3], cube[:, :, :, 0], cube[:, :, :, 3]]
    return [piece.reshape(144, count_elems) for piece in slices]

def lift_faces(volume, corrections):
    count_elems = volume.shape[-1]
    shaped = [piece.reshape(9, 4, 4, count_elems) for piece in corrections]
    zero_face = jnp.zeros_like(shaped[0])
    along_first = jnp.stack([shaped[0], zero_face, zero_face, shaped[1]], axis=1)
    along_second = jnp.stack([shaped[2], zero_face, zero_face, shaped[3]], axis=2)
    along_third = jnp.stack([shaped[4], zero_face, zero_face, shaped[5]], axis=3)
    cube = volume.reshape(9, 4, 4, 4, count_elems) + along_first + along_second + along_third
    return cube.reshape(9, 64, count_elems)

def predict(nodal_field, material, gradient_scale):
    terms = [nodal_field]
    for order_index in range(ORDER - 1):
        terms.append(volume_rate(terms[-1], material, gradient_scale))
    return terms

def taylor(terms, start, stop):
    total = None
    for order_index in range(len(terms)):
        weight = (stop ** (order_index + 1) - start ** (order_index + 1)) / math.factorial(order_index + 1)
        total = terms[order_index] * weight if total is None else total + terms[order_index] * weight
    return total

def halo_source(traces):
    count_elems = traces[0].shape[1]
    lower_half = jnp.arange(count_elems)[None, :] < count_elems // 2
    return jnp.where(lower_half, traces[4], traces[5])

def correct(nodal_field, integral, traces, material, links, halo_lower, halo_upper, interface, gradient_scale):
    volume_change = volume_rate(integral, material, gradient_scale)
    zero_trace = jnp.zeros_like(traces[0]).reshape(9, 16, -1)
    corrections = []
    for face_index in range(6):
        trace_table = jnp.concatenate([traces[face_index ^ 1], halo_lower, halo_upper, interface], axis=1)
        outer_trace = jnp.take(trace_table, links[face_index], axis=1)
        jump_trace = (outer_trace - traces[face_index]).reshape(9, 16, -1)
        signed = jump_trace if face_index % 2 else -jump_trace
        spatial_gradients = [zero_trace, zero_trace, zero_trace]
        spatial_gradients[face_index // 2] = signed
        normal = stress_rates(spatial_gradients[0], spatial_gradients[1], spatial_gradients[2], material)
        corrections.append(((normal + material[3] * jump_trace) * (0.5 * lift_weight * gradient_scale)).reshape(144, -1))
    return lift_faces(nodal_field + volume_change, corrections)

def face_columns(nodal_field, columns):
    return jnp.take(jnp.concatenate(face_traces(nodal_field), axis=1), columns, axis=1)

def source_field(source_elem, source_amp, source_shape, count_elems):
    onehot = (source_elem[:, None] == jnp.arange(count_elems)[None, :]).astype(jnp.float32)
    pattern = (source_amp[:, None, :] * source_shape[None, :, :]).reshape(9 * 64, -1)
    return (coarse_dt * jnp.dot(pattern, onehot, precision=highest_order)).reshape(9, 64, count_elems)

def per_device(array, width):
    moved = array.reshape(array.shape[:-1] + (NDEV, width))
    return jnp.moveaxis(moved, -2, 0)

def to_global(array):
    moved = jnp.moveaxis(array, 0, -2)
    return moved.reshape(moved.shape[:-2] + (moved.shape[-2] * moved.shape[-1],))

def across_sub(buffers):
    groups = NDEV // N_SUB
    count_terms = buffers.shape[1]
    shaped = buffers.reshape(groups, N_SUB, count_terms, 144, N_SUB, SLOT)
    return jnp.transpose(shaped, (0, 4, 2, 3, 1, 5)).reshape(NDEV, count_terms, 144, IFACE)

def advance_all(nodal_field, integral, material, links, interface, gradient_scale):
    traces = jax.vmap(face_traces)(integral)
    source = jax.vmap(halo_source)(traces)
    halo_lower = jnp.roll(source, 1, axis=0)[:, :, ELEMS - LAYER:]
    halo_upper = jnp.roll(source, -1, axis=0)[:, :, :LAYER]
    return jax.vmap(partial(correct, gradient_scale=gradient_scale))(nodal_field, integral, traces, material, links, halo_lower, halo_upper, interface)

def reference(coarse_state, fine_nodal_state, coarse_elastic, coarse_density, fine_lame_shear, fine_density, coarse_links, fine_links, coarse_send, fine_return, source_elem, source_amp, source_shape):
    fine_dt = coarse_dt / SUBSTEPS
    coarse_field = per_device(coarse_state, ELEMS)
    fine_field = per_device(fine_nodal_state, ELEMS)
    coarse_material = jax.vmap(make_material)(per_device(coarse_elastic, ELEMS), per_device(coarse_density, ELEMS))
    fine_material = jax.vmap(make_material)(per_device(fine_lame_shear, ELEMS), per_device(fine_density, ELEMS))
    coarse_table = per_device(coarse_links, ELEMS)
    fine_table = per_device(fine_links, ELEMS)
    send_columns = coarse_send.reshape(NDEV, IFACE)
    return_columns = fine_return.reshape(NDEV, IFACE)
    sources = jax.vmap(partial(source_field, count_elems=ELEMS))(source_elem.reshape(NDEV, SRC), per_device(source_amp, SRC), per_device(source_shape, SRC))
    for step_index in range(STEPS):
        coarse_terms = jax.vmap(partial(predict, gradient_scale=coarse_scale))(coarse_field, coarse_material)
        coarse_integral = taylor(coarse_terms, 0.0, coarse_dt)
        sent = []
        for sub_index in range(SUBSTEPS):
            part_integral = taylor(coarse_terms, sub_index * fine_dt, (sub_index + 1) * fine_dt)
            sent.append(jax.vmap(face_columns)(part_integral, send_columns))
        received = across_sub(jnp.stack(sent, axis=1))
        returned = None
        for sub_index in range(SUBSTEPS):
            fine_terms = jax.vmap(partial(predict, gradient_scale=fine_scale))(fine_field, fine_material)
            fine_integral = taylor(fine_terms, 0.0, fine_dt)
            fine_field = advance_all(fine_field, fine_integral, fine_material, fine_table, received[:, sub_index], fine_scale)
            piece_back = jax.vmap(face_columns)(fine_integral, return_columns)
            returned = piece_back if returned is None else returned + piece_back
        back = across_sub(returned[:, None])[:, 0]
        coarse_field = advance_all(coarse_field, coarse_integral, coarse_material, coarse_table, back, coarse_scale) + sources
    return (to_global(coarse_field), to_global(fine_field))
```

```python
import math

import jax
import jax.numpy as jnp
import numpy as np
from jax import lax
from jax.experimental import pallas as pl
from jax.experimental.pallas import tpu as pltpu
from jax.sharding import PartitionSpec as P

MESH = pl.DeviceIdType.MESH
COARSE_DT = 0.03
FINE_DT = 0.015
F32 = jnp.float32
BF16 = jnp.bfloat16


def derivative_tables():
    points = np.array([-1.0, -1.0 / math.sqrt(5.0), 1.0 / math.sqrt(5.0), 1.0])
    bary = np.array([1.0 / np.prod([points[c] - points[o] for o in range(4) if o != c]) for c in range(4)])
    d = np.zeros((4, 4))
    for r in range(4):
        for c in range(4):
            if r != c:
                d[r, c] = bary[c] / bary[r] / (points[r] - points[c])
        d[r, r] = -np.sum(d[r])
    eye = np.eye(4)
    along_x = np.kron(d, np.eye(16))
    along_y = np.kron(np.kron(eye, d), eye)
    along_z = np.kron(np.eye(16), d)
    full = np.concatenate([along_x, along_y, along_z]).astype(np.float32)
    high = full.astype(BF16)
    low = (full - high.astype(np.float32)).astype(BF16)
    return np.concatenate([high, low, high], axis=1)


def kernel(n_dom, n_sub, *refs):
    (qc_hbm, qf_hbm, cel, cden, fel, fden, clinks, flinks, csend, fret, selem, samp, sshape, dmat,
     outc_hbm, outf_hbm,
     qc, qf, cur, ic, if_, c0, base_c, base_f, rhs, grads, tc, t0, tf, jc, jf, tab_h, tab_i, ret0,
     hs, hr, xs, xr, in_sem, out_sem, hs_sem, hr_sem, xs_sem, xr_sem) = refs

    dom, sub = lax.axis_index("dom"), lax.axis_index("sub")
    n_all = n_dom * n_sub
    here = dom * n_sub + sub
    above, below = lax.rem(here + 1, n_all), lax.rem(here + n_all - 1, n_all)
    above_id = (above // n_sub, lax.rem(above, n_sub))
    below_id = (below // n_sub, lax.rem(below, n_sub))

    load_f = pltpu.make_async_copy(qf_hbm, qf, in_sem.at[0])
    load_c = pltpu.make_async_copy(qc_hbm, qc, in_sem.at[1])
    load_f.start()
    load_c.start()

    barrier = pltpu.get_barrier_semaphore()
    for d in range(1, n_sub):
        pl.semaphore_signal(barrier, inc=1, device_id=(dom, lax.rem(sub + d, n_sub)), device_id_type=MESH)
    for peer in (above_id, below_id):
        pl.semaphore_signal(barrier, inc=1, device_id=peer, device_id_type=MESH)

    lane = lax.broadcasted_iota(jnp.int32, (1, 128), 1)
    lane_lo = lane < 64
    sub_lo = lax.broadcasted_iota(jnp.int32, (8, 1), 0) < 4

    def material(el, den, g):
        lame, shear = el[0:1, :], el[1:2, :]
        buoy = 1.0 / den[...].reshape(1, 128)
        speed = jnp.sqrt((lame + 2.0 * shear) * buoy)
        return lame * g, shear * g, buoy * g, speed * g

    mat_c, mat_f = material(cel, cden, 1.0), material(fel, fden, 2.0)

    def rates(src, mat, emit):
        for v in range(9):
            x = src[64 * v : 64 * v + 64, :]
            high = x.astype(BF16)
            low = (x - high.astype(F32)).astype(BF16)
            at = slice(128 * v, 128 * v + 128)
            rhs[0:64, at] = high
            rhs[64:128, at] = high
            rhs[128:192, at] = low
        grads[...] = jnp.dot(dmat[...], rhs[...], preferred_element_type=F32)
        lame, shear, buoy, _ = mat

        def gr(axis, v):
            return grads[64 * axis : 64 * axis + 64, 128 * v : 128 * v + 128]

        x6, y7, z8 = gr(0, 6), gr(1, 7), gr(2, 8)
        spread = lame * (x6 + y7 + z8)
        shear2 = 2.0 * shear
        emit(0, spread + shear2 * x6)
        emit(1, spread + shear2 * y7)
        emit(2, spread + shear2 * z8)
        emit(3, shear * (gr(1, 6) + gr(0, 7)))
        emit(4, shear * (gr(2, 7) + gr(1, 8)))
        emit(5, shear * (gr(2, 6) + gr(0, 8)))
        emit(6, buoy * (gr(0, 0) + gr(1, 3) + gr(2, 5)))
        emit(7, buoy * (gr(0, 3) + gr(1, 1) + gr(2, 4)))
        emit(8, buoy * (gr(0, 5) + gr(1, 4) + gr(2, 2)))

    def predictor(src, mat, targets):
        cur[...] = src[...]
        for ref, dt in targets:
            ref[...] = src[...] * dt

        def order(k, weights):
            shrink = jnp.where(k == 0, 1.0 / 2.0, jnp.where(k == 1, 1.0 / 3.0, 1.0 / 4.0)).astype(F32)
            weights = tuple(w * (shrink * dt) for w, (_, dt) in zip(weights, targets))

            def emit(v, value):
                at = slice(64 * v, 64 * v + 64)
                cur[at, :] = value
                for (ref, _), w in zip(targets, weights):
                    ref[at, :] = ref[at, :] + w * value

            rates(cur, mat, emit)
            return weights

        lax.fori_loop(0, 3, order, tuple(jnp.float32(dt) for _, dt in targets))

    def traces(src, out):
        for v in range(9):
            out[16 * v : 16 * v + 16, :] = src[64 * v : 64 * v + 16, :]
            out[144 + 16 * v : 160 + 16 * v, :] = src[64 * v + 48 : 64 * v + 64, :]
        blocks = src[...].reshape(18, 2, 16, 128)
        even, odd = blocks[:, 0, 0:8], blocks[:, 1, 0:8]
        out[288:432, :] = jnp.where(sub_lo[None], even, pltpu.roll(odd, 4, 1)).reshape(144, 128)
        even, odd = blocks[:, 0, 8:16], blocks[:, 1, 8:16]
        out[432:576, :] = jnp.where(sub_lo[None], pltpu.roll(even, 4, 1), odd).reshape(144, 128)
        out[576:720, :] = src[pl.ds(0, 144, stride=4), :]
        out[720:864, :] = src[pl.ds(3, 144, stride=4), :]

    def gather(table, index):
        return jnp.take_along_axis(table, jnp.broadcast_to(index, table.shape), axis=1, mode="promise_in_bounds")

    def face(ref, f):
        return ref[144 * f : 144 * f + 144, :]

    def face_columns(ref, columns):
        index, which = columns & 127, columns >> 7
        total = gather(face(ref, 0), index)
        for f in range(1, 6):
            total = jnp.where(which == f, gather(face(ref, f), index), total)
        return total

    block = lane >> 4

    def butterfly(parts):
        for step in (1, 2, 4):
            keep = (block & step) == 0
            fresh = list(parts)
            for i in range(8):
                if not i & step:
                    low, high = parts[i], parts[i + step]
                    fresh[i] = jnp.where(keep, low, pltpu.roll(high, 16 * step, 1))
                    fresh[i + step] = jnp.where(keep, pltpu.roll(low, 128 - 16 * step, 1), high)
            parts = fresh
        return parts

    def exchange_copy(phase, d):
        peer = lax.rem(sub + d, n_sub)
        return pltpu.make_async_remote_copy(
            src_ref=xs.at[phase, peer], dst_ref=xr.at[phase, sub],
            send_sem=xs_sem.at[phase, d - 1], recv_sem=xr_sem.at[phase, d - 1],
            device_id=(dom, peer), device_id_type=MESH)

    def exchange_start(phase, value):
        parts = [value[24 * i : 24 * i + 24, :] for i in range(6)]
        parts = butterfly(parts + [parts[0], parts[0]])
        for b in range(8):
            xs[phase, b] = parts[b]
        for d in range(1, n_sub):
            exchange_copy(phase, d).start()

    def exchange_wait(phase):
        for d in range(1, n_sub):
            origin = lax.rem(sub + n_sub - d, n_sub)
            pltpu.make_async_remote_copy(
                src_ref=xs.at[phase, origin], dst_ref=xr.at[phase, origin],
                send_sem=xs_sem.at[phase, d - 1], recv_sem=xr_sem.at[phase, d - 1],
                device_id=(dom, origin), device_id_type=MESH).wait_recv()

    def exchange_read(phase):
        xr[phase, sub] = xs[phase, sub]
        parts = butterfly([xr[phase, a] for a in range(8)])
        return jnp.concatenate(parts[:6], axis=0)

    def halo_copies(phase):
        return [
            pltpu.make_async_remote_copy(
                src_ref=hs.at[phase, way], dst_ref=hr.at[phase, way],
                send_sem=hs_sem.at[phase, way], recv_sem=hr_sem.at[phase, way],
                device_id=peer, device_id_type=MESH)
            for way, peer in enumerate((above_id, below_id))]

    def halo_pack(phase, ref):
        low, high = ref[720:792, :], ref[792:864, :]
        hs[phase, 0] = jnp.where(lane_lo, pltpu.roll(low, 64, 1), high)
        low, high = ref[576:648, :], ref[648:720, :]
        hs[phase, 1] = jnp.where(lane_lo, low, pltpu.roll(high, 64, 1))

    def halo_start(phase):
        for copy in halo_copies(phase):
            copy.start()

    def halo_wait(phase):
        for copy in halo_copies(phase):
            copy.wait_recv()

    def halo_read(phase):
        lower, upper = hr[phase, 0], hr[phase, 1]
        tab_h[0:72, :] = jnp.where(lane_lo, lower, pltpu.roll(upper, 64, 1))
        tab_h[72:144, :] = jnp.where(lane_lo, pltpu.roll(lower, 64, 1), upper)

    def pick(links, f, table, low):
        row = links[f : f + 1, :]
        hit = (row >= low) & (row < low + 128)
        return jnp.where(hit, gather(table, row & 127), 0.0)

    def jump_own(links, t, j):
        for f in range(6):
            j[144 * f : 144 * f + 144, :] = pick(links, f, face(t, f ^ 1), 0) - face(t, f)

    def jump_add(links, j, table, low):
        for f in range(6):
            j[144 * f : 144 * f + 144, :] = face(j, f) + pick(links, f, table[...], low)

    def lift(mat, j, base, extra):
        lame, shear, buoy, speed = [3.0 * m for m in mat]
        full = lame + 2.0 * shear
        normal = (6, 7, 8)
        stress = ((0, 3, 5), (3, 1, 4), (5, 4, 2))
        for f in range(6):
            axis, sign = f // 2, 1.0 if f % 2 else -1.0
            jump = face(j, f)
            for links, table, low in extra:
                jump = jump + pick(links, f, table[...], low)
            part = [jump[16 * v : 16 * v + 16, :] for v in range(9)]
            vel = part[normal[axis]]
            lam_s, full_s, shear_s, buoy_s = sign * lame, sign * full, sign * shear, sign * buoy
            out = [None] * 9
            for v in range(3):
                out[v] = speed * part[v] + (full_s if v == axis else lam_s) * vel
            pairs = {3: (0, 1), 4: (1, 2), 5: (0, 2)}
            for v, (a, b) in pairs.items():
                out[v] = speed * part[v]
                if axis in (a, b):
                    out[v] = out[v] + shear_s * part[6 + (b if axis == a else a)]
            for v in range(3):
                out[6 + v] = speed * part[6 + v] + buoy_s * part[stress[axis][v]]
            if axis == 0:
                for v in range(9):
                    at = slice(64 * v + 48 * (f % 2), 64 * v + 48 * (f % 2) + 16)
                    base[at, :] = base[at, :] + out[v]
            elif axis == 1:
                for v in range(9):
                    for p in range(2):
                        c = out[v][8 * p : 8 * p + 8, :]
                        r = pltpu.roll(c, 4, 0)
                        at = 64 * v + 32 * p + 8 * (f % 2)
                        if f % 2:
                            first, second = jnp.where(sub_lo, 0.0, r), jnp.where(sub_lo, 0.0, c)
                        else:
                            first, second = jnp.where(sub_lo, c, 0.0), jnp.where(sub_lo, r, 0.0)
                        base[at : at + 8, :] = base[at : at + 8, :] + first
                        base[at + 16 : at + 24, :] = base[at + 16 : at + 24, :] + second
            else:
                for v in range(9):
                    at = pl.ds(64 * v + 3 * (f % 2), 16, stride=4)
                    base[at, :] = base[at, :] + out[v]

    def start_base(q, integral, mat, base):
        def emit(v, value):
            at = slice(64 * v, 64 * v + 64)
            base[at, :] = q[at, :] + value

        rates(integral, mat, emit)

    send_row = csend[...].reshape(1, 128)
    return_row = fret[...].reshape(1, 128)

    load_f.wait()
    predictor(qf, mat_f, ((if_, FINE_DT),))
    traces(if_, tf)
    halo_pack(0, tf)
    pl.semaphore_wait(barrier, n_sub + 1)
    halo_start(0)

    load_c.wait()
    predictor(qc, mat_c, ((c0, FINE_DT), (ic, COARSE_DT)))
    traces(c0, t0)
    first = face_columns(t0, send_row)
    exchange_start(0, first)

    traces(ic, tc)
    second = face_columns(tc, send_row) - first
    halo_pack(1, tc)
    start_base(qf, if_, mat_f, base_f)
    jump_own(flinks, tf, jf)
    ret0[...] = face_columns(tf, return_row)

    halo_wait(0)
    halo_read(0)
    exchange_wait(0)
    tab_i[...] = exchange_read(0)
    exchange_start(1, second)
    halo_start(1)
    lift(mat_f, jf, base_f, ((flinks, tab_h, 128), (flinks, tab_i, 256)))

    predictor(base_f, mat_f, ((if_, FINE_DT),))
    traces(if_, tf)
    halo_pack(2, tf)
    halo_start(2)
    exchange_start(2, ret0[...] + face_columns(tf, return_row))

    start_base(base_f, if_, mat_f, qf)
    jump_own(flinks, tf, jf)
    start_base(qc, ic, mat_c, base_c)
    jump_own(clinks, tc, jc)
    node_of = sshape[...]
    rows = lax.broadcasted_iota(jnp.int32, (4, 128), 0)
    lanes = lax.broadcasted_iota(jnp.int32, (4, 128), 1)
    for v in range(9):
        spots = jnp.zeros((4, 128), F32)
        for i in range(4):
            spots = jnp.where((rows == i) & (lanes == selem[i]), COARSE_DT * samp[i, v], spots)
        field = lax.dot_general(node_of, spots, (((0,), (0,)), ((), ())), precision=lax.Precision.HIGHEST,
                                preferred_element_type=F32)
        base_c[64 * v : 64 * v + 64, :] = base_c[64 * v : 64 * v + 64, :] + field
    exchange_wait(1)
    tab_i[...] = exchange_read(1)
    jump_add(flinks, jf, tab_i, 256)
    halo_wait(1)
    halo_read(1)
    jump_add(clinks, jc, tab_h, 128)

    exchange_wait(2)
    tab_i[...] = exchange_read(2)
    lift(mat_c, jc, base_c, ((clinks, tab_i, 256),))
    store_c = pltpu.make_async_copy(base_c, outc_hbm, out_sem.at[0])
    store_c.start()
    halo_wait(2)
    halo_read(2)
    lift(mat_f, jf, qf, ((flinks, tab_h, 128),))
    store_f = pltpu.make_async_copy(qf, outf_hbm, out_sem.at[1])
    store_f.start()

    for phase in range(3):
        for copy in halo_copies(phase):
            copy.wait_send()
        for d in range(1, n_sub):
            exchange_copy(phase, d).wait_send()
    store_c.wait()
    store_f.wait()


def per_device(n_dom, n_sub, coarse, fine, cel, cden, fel, fden, clinks, flinks, csend, fret, selem, samp, sshape):
    hbm = pl.BlockSpec(memory_space=pl.ANY)
    vmem = pl.BlockSpec(memory_space=pltpu.VMEM)
    smem = pl.BlockSpec(memory_space=pltpu.SMEM)
    field = pltpu.VMEM((576, 128), F32)
    faces = pltpu.VMEM((864, 128), F32)
    trace = pltpu.VMEM((144, 128), F32)
    out = jax.ShapeDtypeStruct((576, 128), F32)

    def body(*refs):
        kernel(n_dom, n_sub, *refs)

    c, f = pl.pallas_call(
        body,
        name="lts",
        out_shape=(out, out),
        in_specs=[hbm, hbm] + [vmem] * 8 + [smem, smem, vmem, vmem],
        out_specs=(hbm, hbm),
        scratch_shapes=[field] * 8
        + [pltpu.VMEM((192, 1152), BF16), pltpu.VMEM((192, 1152), F32)]
        + [faces] * 5
        + [trace] * 3
        + [pltpu.VMEM((3, 2, 72, 128), F32)] * 2
        + [pltpu.VMEM((3, 8, 24, 128), F32)] * 2
        + [pltpu.SemaphoreType.DMA((2,))] * 2
        + [pltpu.SemaphoreType.DMA((3, 2))] * 2
        + [pltpu.SemaphoreType.DMA((3, 7))] * 2,
        compiler_params=pltpu.CompilerParams(collective_id=0, has_side_effects=True),
    )(coarse.reshape(576, 128), fine.reshape(576, 128), cel, cden, fel, fden, clinks, flinks, csend, fret,
      selem, samp.T, sshape.T, jnp.asarray(derivative_tables()))
    return c.reshape(9, 64, 128), f.reshape(9, 64, 128)


def solution(mesh):
    n_dom, n_sub = mesh.shape["dom"], mesh.shape["sub"]
    every = ("dom", "sub")

    def body(*args):
        return per_device(n_dom, n_sub, *args)

    return jax.shard_map(
        body,
        mesh=mesh,
        in_specs=(
            P(None, None, every), P(None, None, every), P(None, every), P(every), P(None, every), P(every),
            P(None, every), P(None, every), P(every), P(every), P(every), P(None, every), P(None, every),
        ),
        out_specs=(P(None, None, every), P(None, None, every)),
        check_vma=False,
    )
```

```python
import math

import jax
import jax.numpy as jnp
import numpy as np
from jax import lax
from jax.experimental import pallas as pl
from jax.experimental.pallas import tpu as pltpu
from jax.sharding import PartitionSpec as P

MESH = pl.DeviceIdType.MESH
COARSE_DT = 0.03
FINE_DT = 0.015
ORDER = (4, 3, 5, 2, 6, 1, 7)
F32 = jnp.float32
BF16 = jnp.bfloat16

def derivative_tables():
    points = np.array([-1.0, -1.0 / math.sqrt(5.0), 1.0 / math.sqrt(5.0), 1.0])
    bary = np.array([1.0 / np.prod([points[c] - points[o] for o in range(4) if o != c]) for c in range(4)])
    d = np.zeros((4, 4))
    for r in range(4):
        for c in range(4):
            if r != c:
                d[r, c] = bary[c] / bary[r] / (points[r] - points[c])
        d[r, r] = -np.sum(d[r])
    eye = np.eye(4)
    along_x = np.kron(d, np.eye(16))
    along_y = np.kron(np.kron(eye, d), eye)
    along_z = np.kron(np.eye(16), d)
    full = np.concatenate([along_x, along_y, along_z, along_x]).astype(np.float32)
    high = full.astype(BF16)
    low = (full - high.astype(np.float32)).astype(BF16)
    return np.concatenate([high, low, high], axis=1)

def kernel(n_dom, n_sub, *refs):
    hbm_refs, (out_c, out_f), vmem_refs = refs[:14], refs[14:16], refs[16:30]
    (qc, qf, cel, cden, fel, fden, clinks, flinks, csend, fret, selem, samp, sshape, dmat) = vmem_refs
    (cur, ic, if_, c0, base_f, tc, t0, tf, jc, jf, tab_h, tab_i, ret0,
     hs, hr, xs, xr, in_sem, hs_sem, hr_sem, xs_sem, xr_sem) = refs[30:]

    dom, sub = lax.axis_index("dom"), lax.axis_index("sub")
    n_all = n_dom * n_sub
    here = dom * n_sub + sub
    above, below = lax.rem(here + 1, n_all), lax.rem(here + n_all - 1, n_all)
    above_id = (above // n_sub, lax.rem(above, n_sub))
    below_id = (below // n_sub, lax.rem(below, n_sub))

    loads = [pltpu.make_async_copy(src, dst, in_sem.at[i]) for i, (src, dst) in enumerate(zip(hbm_refs, vmem_refs))]
    early = (1, 4, 5, 13)
    late = (0, 2, 3, 8, 7, 9, 6, 10, 11, 12)
    for i in early:
        loads[i].start()

    barrier = pltpu.get_barrier_semaphore()
    for d in range(1, n_sub):
        pl.semaphore_signal(barrier, inc=1, device_id=(dom, lax.rem(sub + d, n_sub)), device_id_type=MESH)
    for peer in (above_id, below_id):
        pl.semaphore_signal(barrier, inc=1, device_id=peer, device_id_type=MESH)

    for i in late:
        loads[i].start()

    lane = lax.broadcasted_iota(jnp.int32, (1, 128), 1)
    lane_lo = lane < 64
    sub_lo = lax.broadcasted_iota(jnp.int32, (8, 1), 0) < 4

    def material(el, den, g):
        lame, shear = el[0:1, :], el[1:2, :]
        buoy = 1.0 / den[...].reshape(1, 128)
        speed = jnp.sqrt((lame + 2.0 * shear) * buoy)
        return lame * g, shear * g, buoy * g, speed * g

    def rates(src, mat, emit):
        lame, shear, buoy, _ = mat

        def along(v, first, last):
            x = src[64 * v : 64 * v + 64, :]
            high = x.astype(BF16)
            low = (x - high.astype(F32)).astype(BF16)
            parts = jnp.dot(dmat[64 * first : 64 * last, :], jnp.concatenate([high, high, low], axis=0),
                            preferred_element_type=F32)
            return [parts[64 * i : 64 * i + 64, :] for i in range(last - first)]

        (x0,), (y1,), (z2,) = along(0, 0, 1), along(1, 1, 2), along(2, 2, 3)
        (x3, y3), (y4, z4), (z5, x5) = along(3, 0, 2), along(4, 1, 3), along(5, 2, 4)
        accel = [buoy * (x0 + y3 + z5), buoy * (x3 + y1 + z4), buoy * (x5 + y4 + z2)]
        (x6, y6, z6), (x7, y7, z7), (x8, y8, z8) = [along(v, 0, 3) for v in (6, 7, 8)]
        spread = lame * (x6 + y7 + z8)
        shear2 = 2.0 * shear
        emit(0, spread + shear2 * x6)
        emit(1, spread + shear2 * y7)
        emit(2, spread + shear2 * z8)
        emit(3, shear * (y6 + x7))
        emit(4, shear * (z7 + y8))
        emit(5, shear * (z6 + x8))
        for v in range(3):
            emit(6 + v, accel[v])

    def predictor(src, mat, targets):
        cur[...] = src[...]
        for ref, dt in targets:
            ref[...] = src[...] * dt

        def order(k, weights):
            shrink = jnp.where(k == 0, 1.0 / 2.0, jnp.where(k == 1, 1.0 / 3.0, 1.0 / 4.0)).astype(F32)
            weights = tuple(w * (shrink * dt) for w, (_, dt) in zip(weights, targets))

            def emit(v, value):
                at = slice(64 * v, 64 * v + 64)
                cur[at, :] = value
                for (ref, _), w in zip(targets, weights):
                    ref[at, :] = ref[at, :] + w * value

            rates(cur, mat, emit)
            return weights

        lax.fori_loop(0, 3, order, tuple(jnp.float32(dt) for _, dt in targets))

    def nested(src, mat, out, dt):
        out[...] = src[...]

        def order(k, _):
            outer = jnp.where(k == 2, dt, 1.0).astype(F32)
            inner = jnp.where(k == 0, dt / 4.0, jnp.where(k == 1, dt / 3.0, dt * dt / 2.0)).astype(F32)

            def emit(v, value):
                at = slice(64 * v, 64 * v + 64)
                out[at, :] = outer * src[at, :] + value

            rates(out, tuple(inner * m for m in mat), emit)
            return 0

        lax.fori_loop(0, 3, order, 0)

    def traces(src, out):
        for v in range(9):
            out[16 * v : 16 * v + 16, :] = src[64 * v : 64 * v + 16, :]
            out[144 + 16 * v : 160 + 16 * v, :] = src[64 * v + 48 : 64 * v + 64, :]
        blocks = src[...].reshape(18, 2, 16, 128)
        even, odd = blocks[:, 0, 0:8], blocks[:, 1, 0:8]
        out[288:432, :] = jnp.where(sub_lo[None], even, pltpu.roll(odd, 4, 1)).reshape(144, 128)
        even, odd = blocks[:, 0, 8:16], blocks[:, 1, 8:16]
        out[432:576, :] = jnp.where(sub_lo[None], pltpu.roll(even, 4, 1), odd).reshape(144, 128)
        out[576:720, :] = src[pl.ds(0, 144, stride=4), :]
        out[720:864, :] = src[pl.ds(3, 144, stride=4), :]

    def gather(table, index):
        return jnp.take_along_axis(table, jnp.broadcast_to(index, table.shape), axis=1, mode="promise_in_bounds")

    def face(ref, f):
        return ref[144 * f : 144 * f + 144, :]

    def face_columns(ref, columns):
        index, which = columns & 127, columns >> 7
        total = gather(face(ref, 0), index)
        for f in range(1, 6):
            total = jnp.where(which == f, gather(face(ref, f), index), total)
        return total

    block = lane >> 4

    def butterfly(parts):
        for step in (1, 2, 4):
            keep = (block & step) == 0
            fresh = list(parts)
            for i in range(8):
                if not i & step:
                    low, high = parts[i], parts[i + step]
                    fresh[i] = jnp.where(keep, low, pltpu.roll(high, 16 * step, 1))
                    fresh[i + step] = jnp.where(keep, pltpu.roll(low, 128 - 16 * step, 1), high)
            parts = fresh
        return parts

    def exchange_copy(phase, d):
        peer = lax.rem(sub + d, n_sub)
        return pltpu.make_async_remote_copy(
            src_ref=xs.at[phase, peer], dst_ref=xr.at[phase, sub],
            send_sem=xs_sem.at[phase, d - 1], recv_sem=xr_sem.at[phase, d - 1],
            device_id=(dom, peer), device_id_type=MESH)

    def exchange_start(phase, value):
        parts = [value[24 * i : 24 * i + 24, :] for i in range(6)]
        parts = butterfly(parts + [parts[0], parts[0]])
        for b in range(8):
            xs[phase, b] = parts[b]
        for d in ORDER:
            exchange_copy(phase, d).start()

    def exchange_wait(phase):
        for d in range(1, n_sub):
            origin = lax.rem(sub + n_sub - d, n_sub)
            pltpu.make_async_remote_copy(
                src_ref=xs.at[phase, origin], dst_ref=xr.at[phase, origin],
                send_sem=xs_sem.at[phase, d - 1], recv_sem=xr_sem.at[phase, d - 1],
                device_id=(dom, origin), device_id_type=MESH).wait_recv()

    def exchange_read(phase):
        xr[phase, sub] = xs[phase, sub]
        parts = butterfly([xr[phase, a] for a in range(8)])
        return jnp.concatenate(parts[:6], axis=0)

    def halo_copies(phase):
        return [
            pltpu.make_async_remote_copy(
                src_ref=hs.at[phase, way], dst_ref=hr.at[phase, way],
                send_sem=hs_sem.at[phase, way], recv_sem=hr_sem.at[phase, way],
                device_id=peer, device_id_type=MESH)
            for way, peer in enumerate((above_id, below_id))]

    def halo_pack(phase, ref):
        low, high = ref[720:792, :], ref[792:864, :]
        hs[phase, 0] = jnp.where(lane_lo, pltpu.roll(low, 64, 1), high)
        low, high = ref[576:648, :], ref[648:720, :]
        hs[phase, 1] = jnp.where(lane_lo, low, pltpu.roll(high, 64, 1))

    def halo_start(phase):
        for copy in halo_copies(phase):
            copy.start()

    def halo_wait(phase):
        for copy in halo_copies(phase):
            copy.wait_recv()

    def halo_read(phase):
        lower, upper = hr[phase, 0], hr[phase, 1]
        tab_h[0:72, :] = jnp.where(lane_lo, lower, pltpu.roll(upper, 64, 1))
        tab_h[72:144, :] = jnp.where(lane_lo, pltpu.roll(lower, 64, 1), upper)

    def pick(links, f, table, low):
        row = links[f : f + 1, :]
        hit = (row >= low) & (row < low + 128)
        return jnp.where(hit, gather(table, row & 127), 0.0)

    def jump_own(links, t, j):
        for f in range(6):
            j[144 * f : 144 * f + 144, :] = pick(links, f, face(t, f ^ 1), 0) - face(t, f)

    def jump_add(links, j, table, low):
        for f in range(6):
            j[144 * f : 144 * f + 144, :] = face(j, f) + pick(links, f, table[...], low)

    def lift(mat, j, base, extra):
        lame, shear, buoy, speed = [3.0 * m for m in mat]
        full = lame + 2.0 * shear
        normal = (6, 7, 8)
        stress = ((0, 3, 5), (3, 1, 4), (5, 4, 2))
        for f in range(6):
            axis, sign = f // 2, 1.0 if f % 2 else -1.0
            jump = face(j, f)
            for links, table, low in extra:
                jump = jump + pick(links, f, table[...], low)
            part = [jump[16 * v : 16 * v + 16, :] for v in range(9)]
            vel = part[normal[axis]]
            lam_s, full_s, shear_s, buoy_s = sign * lame, sign * full, sign * shear, sign * buoy
            out = [None] * 9
            for v in range(3):
                out[v] = speed * part[v] + (full_s if v == axis else lam_s) * vel
            pairs = {3: (0, 1), 4: (1, 2), 5: (0, 2)}
            for v, (a, b) in pairs.items():
                out[v] = speed * part[v]
                if axis in (a, b):
                    out[v] = out[v] + shear_s * part[6 + (b if axis == a else a)]
            for v in range(3):
                out[6 + v] = speed * part[6 + v] + buoy_s * part[stress[axis][v]]
            if axis == 0:
                for v in range(9):
                    at = slice(64 * v + 48 * (f % 2), 64 * v + 48 * (f % 2) + 16)
                    base[at, :] = base[at, :] + out[v]
            elif axis == 1:
                for v in range(9):
                    for p in range(2):
                        c = out[v][8 * p : 8 * p + 8, :]
                        r = pltpu.roll(c, 4, 0)
                        at = 64 * v + 32 * p + 8 * (f % 2)
                        if f % 2:
                            first, second = jnp.where(sub_lo, 0.0, r), jnp.where(sub_lo, 0.0, c)
                        else:
                            first, second = jnp.where(sub_lo, c, 0.0), jnp.where(sub_lo, r, 0.0)
                        base[at : at + 8, :] = base[at : at + 8, :] + first
                        base[at + 16 : at + 24, :] = base[at + 16 : at + 24, :] + second
            else:
                for v in range(9):
                    at = pl.ds(64 * v + 3 * (f % 2), 16, stride=4)
                    base[at, :] = base[at, :] + out[v]

    def start_base(q, integral, mat, base):
        def emit(v, value):
            at = slice(64 * v, 64 * v + 64)
            base[at, :] = q[at, :] + value

        rates(integral, mat, emit)

    for i in early:
        loads[i].wait()
    mat_f = material(fel, fden, 2.0)
    nested(qf, mat_f, if_, FINE_DT)
    traces(if_, tf)

    halo_pack(0, tf)
    pl.semaphore_wait(barrier, n_sub + 1)
    halo_start(0)

    for i in late:
        loads[i].wait()
    mat_c = material(cel, cden, 1.0)
    send_row = csend[...].reshape(1, 128)
    return_row = fret[...].reshape(1, 128)
    predictor(qc, mat_c, ((c0, FINE_DT), (ic, COARSE_DT)))
    traces(c0, t0)

    first = face_columns(t0, send_row)
    exchange_start(0, first)

    traces(ic, tc)
    second = face_columns(tc, send_row) - first
    halo_pack(1, tc)
    start_base(qf, if_, mat_f, base_f)
    jump_own(flinks, tf, jf)
    ret0[...] = face_columns(tf, return_row)

    halo_wait(0)
    halo_read(0)
    exchange_wait(0)
    tab_i[...] = exchange_read(0)
    exchange_start(1, second)
    halo_start(1)

    lift(mat_f, jf, base_f, ((flinks, tab_h, 128), (flinks, tab_i, 256)))

    nested(base_f, mat_f, if_, FINE_DT)
    traces(if_, tf)

    halo_pack(2, tf)
    halo_start(2)
    exchange_start(2, ret0[...] + face_columns(tf, return_row))

    start_base(base_f, if_, mat_f, out_f)
    jump_own(flinks, tf, jf)
    start_base(qc, ic, mat_c, out_c)
    jump_own(clinks, tc, jc)
    node_of, amp = sshape[...], COARSE_DT * samp[...]
    square = lax.broadcasted_iota(jnp.int32, (4, 4), 0) == lax.broadcasted_iota(jnp.int32, (4, 4), 1)
    spot = selem[...].astype(F32).reshape(1, 4)
    column = jnp.sum(jnp.where(square, spot, 0.0), axis=1, keepdims=True)
    hit = lane.astype(F32) == column
    for v in range(9):
        field = lax.dot_general(node_of, jnp.where(hit, amp[:, v : v + 1], 0.0), (((0,), (0,)), ((), ())),
                                precision=lax.Precision.HIGHEST, preferred_element_type=F32)
        out_c[64 * v : 64 * v + 64, :] = out_c[64 * v : 64 * v + 64, :] + field

    exchange_wait(1)
    tab_i[...] = exchange_read(1)
    jump_add(flinks, jf, tab_i, 256)
    halo_wait(1)
    halo_read(1)
    jump_add(clinks, jc, tab_h, 128)

    halo_wait(2)
    halo_read(2)
    lift(mat_f, jf, out_f, ((flinks, tab_h, 128),))

    exchange_wait(2)
    tab_i[...] = exchange_read(2)
    lift(mat_c, jc, out_c, ((clinks, tab_i, 256),))

    for phase in range(3):
        for copy in halo_copies(phase):
            copy.wait_send()
        for d in ORDER:
            exchange_copy(phase, d).wait_send()

def store(c_ref, f_ref, outc_ref, outf_ref, sem):
    copies = [pltpu.make_async_copy(src, dst, sem.at[i]) for i, (src, dst) in enumerate(((c_ref, outc_ref), (f_ref, outf_ref)))]
    for piece in copies:
        piece.start()
    for piece in copies:
        piece.wait()

def per_device(n_dom, n_sub, coarse, fine, cel, cden, fel, fden, clinks, flinks, csend, fret, selem, samp, sshape):
    hbm = pl.BlockSpec(memory_space=pl.ANY)
    vmem = pl.BlockSpec(memory_space=pltpu.VMEM)
    field = pltpu.VMEM((576, 128), F32)
    faces = pltpu.VMEM((864, 128), F32)
    trace = pltpu.VMEM((144, 128), F32)
    out = jax.ShapeDtypeStruct((576, 128), F32)

    def body(*refs):
        kernel(n_dom, n_sub, *refs)

    args = (coarse.reshape(576, 128), fine.reshape(576, 128), cel, cden, fel, fden, clinks, flinks, csend, fret,
            selem, samp.T, sshape.T, jnp.asarray(derivative_tables()))
    c, f = pl.pallas_call(
        body,
        name="lts",
        out_shape=(pltpu.VMEM((576, 128), F32), pltpu.VMEM((576, 128), F32)),
        in_specs=[hbm] * 14,
        out_specs=(vmem, vmem),
        scratch_shapes=[pltpu.VMEM(a.shape, a.dtype) for a in args]
        + [field] * 5
        + [faces] * 5
        + [trace] * 3
        + [pltpu.VMEM((3, 2, 72, 128), F32)] * 2
        + [pltpu.VMEM((3, 8, 24, 128), F32)] * 2
        + [pltpu.SemaphoreType.DMA((14,))]
        + [pltpu.SemaphoreType.DMA((3, 2))] * 2
        + [pltpu.SemaphoreType.DMA((3, 7))] * 2,
        compiler_params=pltpu.CompilerParams(collective_id=0, has_side_effects=True),
    )(*args)
    c, f = pl.pallas_call(
        store,
        name="put",
        out_shape=(out, out),
        in_specs=[vmem, vmem],
        out_specs=(hbm, hbm),
        scratch_shapes=[pltpu.SemaphoreType.DMA((2,))],
    )(pltpu.with_memory_space_constraint(c, pltpu.VMEM), pltpu.with_memory_space_constraint(f, pltpu.VMEM))
    return c.reshape(9, 64, 128), f.reshape(9, 64, 128)

def solution(mesh):
    n_dom, n_sub = mesh.shape["dom"], mesh.shape["sub"]
    every = ("dom", "sub")

    def body(*args):
        return per_device(n_dom, n_sub, *args)

    return jax.shard_map(
        body,
        mesh=mesh,
        in_specs=(
            P(None, None, every), P(None, None, every), P(None, every), P(every), P(None, every), P(every),
            P(None, every), P(None, every), P(every), P(every), P(every), P(None, every), P(None, every),
        ),
        out_specs=(P(None, None, every), P(None, None, every)),
        check_vma=False,
    )
```

```python
import math

import jax
import jax.numpy as jnp
import numpy as np
from jax import lax
from jax.experimental import pallas as pl
from jax.experimental.pallas import tpu as pltpu
from jax.sharding import PartitionSpec as P

MESH = pl.DeviceIdType.MESH
COARSE_DT = 0.03
FINE_DT = 0.015
ORDER = (4, 3, 5, 2, 6, 1, 7)
F32 = jnp.float32
BF16 = jnp.bfloat16

def derivative():
    points = np.array([-1.0, -1.0 / math.sqrt(5.0), 1.0 / math.sqrt(5.0), 1.0])
    bary = np.array([1.0 / np.prod([points[c] - points[o] for o in range(4) if o != c]) for c in range(4)])
    d = np.zeros((4, 4))
    for r in range(4):
        for c in range(4):
            if r != c:
                d[r, c] = bary[c] / bary[r] / (points[r] - points[c])
        d[r, r] = -np.sum(d[r])
    return d

def derivative_tables():
    d, eye = derivative(), np.eye(4)
    along_y = np.kron(np.kron(eye, d), eye)
    along_z = np.kron(np.eye(16), d)
    full = np.concatenate([along_y, along_z]).astype(np.float32)
    high = full.astype(BF16)
    low = (full - high.astype(np.float32)).astype(BF16)
    return np.concatenate([high, low, high], axis=1)

def kernel(n_dom, n_sub, *refs):
    hbm_refs, (out_c, out_f), vmem_refs = refs[:14], refs[14:16], refs[16:30]
    (qc, qf, cel, cden, fel, fden, clinks, flinks, csend, fret, selem, samp, sshape, dmat) = vmem_refs
    (ic, if_, c0, base_f, tc, t0, tf, jc, jf, tab_h, tab_i, ret0,
     hs, hr, xs, xr, in_sem, hs_sem, hr_sem, xs_sem, xr_sem) = refs[30:]

    dom, sub = lax.axis_index("dom"), lax.axis_index("sub")
    n_all = n_dom * n_sub
    here = dom * n_sub + sub
    above, below = lax.rem(here + 1, n_all), lax.rem(here + n_all - 1, n_all)
    above_id = (above // n_sub, lax.rem(above, n_sub))
    below_id = (below // n_sub, lax.rem(below, n_sub))

    barrier = pltpu.get_barrier_semaphore()
    for peer in (below_id, above_id):
        pl.semaphore_signal(barrier, inc=1, device_id=peer, device_id_type=MESH)
    for d in ORDER:
        pl.semaphore_signal(barrier, inc=1, device_id=(dom, lax.rem(sub + d, n_sub)), device_id_type=MESH)

    loads = [pltpu.make_async_copy(src, dst, in_sem.at[i]) for i, (src, dst) in enumerate(zip(hbm_refs, vmem_refs))]
    early = (1, 0, 4, 5, 2, 3, 13)
    late = (8, 7, 9, 6, 10, 11, 12)
    for i in early:
        loads[i].start()
    for i in late:
        loads[i].start()

    lane = lax.broadcasted_iota(jnp.int32, (1, 128), 1)
    lane_lo = lane < 64
    sub_lo = lax.broadcasted_iota(jnp.int32, (8, 1), 0) < 4

    def material(el, den, g):
        lame, shear = el[0:1, :], el[1:2, :]
        buoy = 1.0 / den[...].reshape(1, 128)
        speed = jnp.sqrt((lame + 2.0 * shear) * buoy)
        return lame * g, shear * g, buoy * g, speed * g

    table = derivative()

    def along_x(x):
        part = [x[16 * i : 16 * i + 16, :] for i in range(4)]
        out = []
        for i in range(4):
            terms = [float(table[i, k]) * part[k] for k in range(4) if abs(table[i, k]) > 1e-9]
            while len(terms) > 1:
                terms = [terms[n] + terms[n + 1] if n + 1 < len(terms) else terms[n] for n in range(0, len(terms), 2)]
            out.append(terms[0])
        return jnp.concatenate(out, axis=0)

    def split(x):
        high = x.astype(BF16)
        low = (x - high.astype(F32)).astype(BF16)
        return jnp.concatenate([high, high, low], axis=0)

    def along(pair, first, last):
        both = jnp.concatenate([split(x) for x in pair], axis=1)
        got = jnp.dot(dmat[64 * first : 64 * last, :], both, preferred_element_type=F32)
        return [[got[64 * i : 64 * i + 64, 128 * k : 128 * k + 128] for i in range(last - first)] for k in range(2)]

    def rates(src, mat, emit):
        lame, shear, buoy, _ = mat
        x = [src[64 * v : 64 * v + 64, :] for v in range(9)]
        (y6, z6), (y7, z7) = along((x[6], x[7]), 0, 2)
        (y8, z8), (y4, z4) = along((x[8], x[4]), 0, 2)
        (y3,), (y1,) = along((x[3], x[1]), 0, 1)
        (z5,), (z2,) = along((x[5], x[2]), 1, 2)
        x6, x7, x8, x0, x3, x5 = [along_x(x[v]) for v in (6, 7, 8, 0, 3, 5)]
        spread = lame * (x6 + y7 + z8)
        shear2 = 2.0 * shear
        out = [spread + shear2 * x6, spread + shear2 * y7, spread + shear2 * z8,
               shear * (y6 + x7), shear * (z7 + y8), shear * (z6 + x8),
               buoy * (x0 + y3 + z5), buoy * (x3 + y1 + z4), buoy * (x5 + y4 + z2)]
        for v in range(9):
            emit(v, out[v])

    def nested(dt, jobs):
        for src, _, out in jobs:
            out[...] = src[...]

        def order(k, _):
            outer = jnp.where(k == 2, dt, 1.0).astype(F32)
            inner = jnp.where(k == 0, dt / 4.0, jnp.where(k == 1, dt / 3.0, dt * dt / 2.0)).astype(F32)
            for src, mat, out in jobs:

                def emit(v, value, src=src, out=out):
                    at = slice(64 * v, 64 * v + 64)
                    out[at, :] = outer * src[at, :] + value

                rates(out, tuple(inner * m for m in mat), emit)
            return 0

        lax.fori_loop(0, 3, order, 0)

    def traces(src, out):
        for v in range(9):
            out[16 * v : 16 * v + 16, :] = src[64 * v : 64 * v + 16, :]
            out[144 + 16 * v : 160 + 16 * v, :] = src[64 * v + 48 : 64 * v + 64, :]
        blocks = src[...].reshape(18, 2, 16, 128)
        even, odd = blocks[:, 0, 0:8], blocks[:, 1, 0:8]
        out[288:432, :] = jnp.where(sub_lo[None], even, pltpu.roll(odd, 4, 1)).reshape(144, 128)
        even, odd = blocks[:, 0, 8:16], blocks[:, 1, 8:16]
        out[432:576, :] = jnp.where(sub_lo[None], pltpu.roll(even, 4, 1), odd).reshape(144, 128)
        out[576:720, :] = src[pl.ds(0, 144, stride=4), :]
        out[720:864, :] = src[pl.ds(3, 144, stride=4), :]

    def gather(table, index):
        return jnp.take_along_axis(table, jnp.broadcast_to(index, table.shape), axis=1, mode="promise_in_bounds")

    def face(ref, f):
        return ref[144 * f : 144 * f + 144, :]

    def face_columns(ref, columns):
        index, which = columns & 127, columns >> 7
        total = gather(face(ref, 0), index)
        for f in range(1, 6):
            total = jnp.where(which == f, gather(face(ref, f), index), total)
        return total

    block = lane >> 4

    def butterfly(parts):
        for step in (1, 2, 4):
            keep = (block & step) == 0
            fresh = list(parts)
            for i in range(8):
                if not i & step:
                    low, high = parts[i], parts[i + step]
                    fresh[i] = jnp.where(keep, low, pltpu.roll(high, 16 * step, 1))
                    fresh[i + step] = jnp.where(keep, pltpu.roll(low, 128 - 16 * step, 1), high)
            parts = fresh
        return parts

    def exchange_copy(phase, d):
        peer = lax.rem(sub + d, n_sub)
        return pltpu.make_async_remote_copy(
            src_ref=xs.at[phase, peer], dst_ref=xr.at[phase, sub],
            send_sem=xs_sem.at[phase], recv_sem=xr_sem.at[phase],
            device_id=(dom, peer), device_id_type=MESH)

    def exchange_start(phase, value):
        exchange_pack(phase, value)
        exchange_send(phase)

    def exchange_pack(phase, value):
        parts = [value[24 * i : 24 * i + 24, :] for i in range(6)]
        parts = butterfly(parts + [parts[0], parts[0]])
        for b in range(8):
            xs[phase, b] = parts[b]

    def exchange_send(phase):
        for d in ORDER:
            exchange_copy(phase, d).start()

    def exchange_all(phase):
        return pltpu.make_async_remote_copy(
            src_ref=xs.at[phase, pl.ds(0, n_sub - 1)], dst_ref=xr.at[phase, pl.ds(0, n_sub - 1)],
            send_sem=xs_sem.at[phase], recv_sem=xr_sem.at[phase],
            device_id=(dom, lax.rem(sub + 1, n_sub)), device_id_type=MESH)

    def exchange_wait(phase):
        exchange_all(phase).wait_recv()

    def exchange_read(phase):
        xr[phase, sub] = xs[phase, sub]
        parts = butterfly([xr[phase, a] for a in range(8)])
        return jnp.concatenate(parts[:6], axis=0)

    def halo_copies(phase):
        return [
            pltpu.make_async_remote_copy(
                src_ref=hs.at[phase, way], dst_ref=hr.at[phase, way],
                send_sem=hs_sem.at[phase], recv_sem=hr_sem.at[phase],
                device_id=peer, device_id_type=MESH)
            for way, peer in enumerate((above_id, below_id))]

    def halo_pack(phase, ref):
        low, high = ref[720:792, :], ref[792:864, :]
        hs[phase, 0] = jnp.where(lane_lo, pltpu.roll(low, 64, 1), high)
        low, high = ref[576:648, :], ref[648:720, :]
        hs[phase, 1] = jnp.where(lane_lo, low, pltpu.roll(high, 64, 1))

    def halo_start(phase):
        for copy in halo_copies(phase):
            copy.start()

    def halo_all(phase):
        return pltpu.make_async_remote_copy(
            src_ref=hs.at[phase], dst_ref=hr.at[phase], send_sem=hs_sem.at[phase], recv_sem=hr_sem.at[phase],
            device_id=above_id, device_id_type=MESH)

    def halo_wait(phase):
        halo_all(phase).wait_recv()

    def halo_read(phase):
        lower, upper = hr[phase, 0], hr[phase, 1]
        tab_h[0:72, :] = jnp.where(lane_lo, lower, pltpu.roll(upper, 64, 1))
        tab_h[72:144, :] = jnp.where(lane_lo, pltpu.roll(lower, 64, 1), upper)

    def pick(links, f, table, low):
        row = links[f : f + 1, :]
        hit = (row >= low) & (row < low + 128)
        return jnp.where(hit, gather(table, row & 127), 0.0)

    def jump_own(links, t, j):
        for f in range(6):
            j[144 * f : 144 * f + 144, :] = pick(links, f, face(t, f ^ 1), 0) - face(t, f)

    def jump_add(links, j, table, low):
        for f in range(6):
            j[144 * f : 144 * f + 144, :] = face(j, f) + pick(links, f, table[...], low)

    def lift(mat, j, base, extra):
        lame, shear, buoy, speed = [3.0 * m for m in mat]
        full = lame + 2.0 * shear
        normal = (6, 7, 8)
        stress = ((0, 3, 5), (3, 1, 4), (5, 4, 2))
        for f in range(6):
            axis, sign = f // 2, 1.0 if f % 2 else -1.0
            jump = face(j, f)
            if len(extra) == 1:
                (links, table_ref, low), = extra
                jump = jump + pick(links, f, table_ref[...], low)
            else:
                row = flinks[f : f + 1, :]
                index = row & 127
                outer = jnp.where(row < 256, gather(tab_h[...], index), gather(tab_i[...], index))
                jump = jump + jnp.where(row < 128, 0.0, outer)
            part = [jump[16 * v : 16 * v + 16, :] for v in range(9)]
            vel = part[normal[axis]]
            lam_s, full_s, shear_s, buoy_s = sign * lame, sign * full, sign * shear, sign * buoy
            out = [None] * 9
            for v in range(3):
                out[v] = speed * part[v] + (full_s if v == axis else lam_s) * vel
            pairs = {3: (0, 1), 4: (1, 2), 5: (0, 2)}
            for v, (a, b) in pairs.items():
                out[v] = speed * part[v]
                if axis in (a, b):
                    out[v] = out[v] + shear_s * part[6 + (b if axis == a else a)]
            for v in range(3):
                out[6 + v] = speed * part[6 + v] + buoy_s * part[stress[axis][v]]
            if axis == 0:
                for v in range(9):
                    at = slice(64 * v + 48 * (f % 2), 64 * v + 48 * (f % 2) + 16)
                    base[at, :] = base[at, :] + out[v]
            elif axis == 1:
                for v in range(9):
                    for p in range(2):
                        c = out[v][8 * p : 8 * p + 8, :]
                        r = pltpu.roll(c, 4, 0)
                        at = 64 * v + 32 * p + 8 * (f % 2)
                        if f % 2:
                            first, second = jnp.where(sub_lo, 0.0, r), jnp.where(sub_lo, 0.0, c)
                        else:
                            first, second = jnp.where(sub_lo, c, 0.0), jnp.where(sub_lo, r, 0.0)
                        base[at : at + 8, :] = base[at : at + 8, :] + first
                        base[at + 16 : at + 24, :] = base[at + 16 : at + 24, :] + second
            else:
                for v in range(9):
                    at = pl.ds(64 * v + 3 * (f % 2), 16, stride=4)
                    base[at, :] = base[at, :] + out[v]

    def start_base(q, integral, mat, base):
        def emit(v, value):
            at = slice(64 * v, 64 * v + 64)
            base[at, :] = q[at, :] + value

        rates(integral, mat, emit)

    for i in early:
        loads[i].wait()
    mat_f = material(fel, fden, 2.0)
    mat_c = material(cel, cden, 1.0)
    nested(FINE_DT, ((qf, mat_f, if_), (qc, mat_c, c0)))

    traces(if_, tf)
    halo_pack(0, tf)
    for i in late:
        loads[i].wait()
    send_row = csend[...].reshape(1, 128)
    return_row = fret[...].reshape(1, 128)
    traces(c0, t0)
    first = face_columns(t0, send_row)
    exchange_pack(0, first)
    pl.semaphore_wait(barrier, n_sub + 1)
    halo_start(0)
    exchange_send(0)

    nested(COARSE_DT, ((qc, mat_c, ic),))
    traces(ic, tc)
    second = face_columns(tc, send_row) - first
    halo_pack(1, tc)
    exchange_start(1, second)
    halo_start(1)
    start_base(qf, if_, mat_f, base_f)
    jump_own(flinks, tf, jf)
    ret0[...] = face_columns(tf, return_row)

    halo_wait(0)
    halo_read(0)
    exchange_wait(0)
    tab_i[...] = exchange_read(0)

    lift(mat_f, jf, base_f, ((flinks, tab_h, 128), (flinks, tab_i, 256)))

    nested(FINE_DT, ((base_f, mat_f, if_),))
    traces(if_, tf)

    halo_pack(2, tf)
    halo_start(2)
    exchange_start(2, ret0[...] + face_columns(tf, return_row))

    start_base(base_f, if_, mat_f, out_f)
    jump_own(flinks, tf, jf)
    start_base(qc, ic, mat_c, out_c)
    jump_own(clinks, tc, jc)
    node_of, amp = sshape[...], COARSE_DT * samp[...]
    square = lax.broadcasted_iota(jnp.int32, (4, 4), 0) == lax.broadcasted_iota(jnp.int32, (4, 4), 1)
    spot = selem[...].astype(F32).reshape(1, 4)
    column = jnp.sum(jnp.where(square, spot, 0.0), axis=1, keepdims=True)
    hit = lane.astype(F32) == column
    for v in range(9):
        field = lax.dot_general(node_of, jnp.where(hit, amp[:, v : v + 1], 0.0), (((0,), (0,)), ((), ())),
                                precision=lax.Precision.HIGHEST, preferred_element_type=F32)
        out_c[64 * v : 64 * v + 64, :] = out_c[64 * v : 64 * v + 64, :] + field

    exchange_wait(1)
    tab_i[...] = exchange_read(1)
    jump_add(flinks, jf, tab_i, 256)
    halo_wait(1)
    halo_read(1)
    jump_add(clinks, jc, tab_h, 128)

    for phase in range(3):
        halo_all(phase).wait_send()
        exchange_all(phase).wait_send()
    halo_wait(2)
    halo_read(2)
    lift(mat_f, jf, out_f, ((flinks, tab_h, 128),))

    exchange_wait(2)
    tab_i[...] = exchange_read(2)
    lift(mat_c, jc, out_c, ((clinks, tab_i, 256),))

def store(c_ref, f_ref, outc_ref, outf_ref, sem):
    copies = [pltpu.make_async_copy(src, dst, sem.at[i]) for i, (src, dst) in enumerate(((c_ref, outc_ref), (f_ref, outf_ref)))]
    for piece in copies:
        piece.start()
    for piece in copies:
        piece.wait()

def per_device(n_dom, n_sub, coarse, fine, cel, cden, fel, fden, clinks, flinks, csend, fret, selem, samp, sshape):
    hbm = pl.BlockSpec(memory_space=pl.ANY)
    vmem = pl.BlockSpec(memory_space=pltpu.VMEM)
    field = pltpu.VMEM((576, 128), F32)
    faces = pltpu.VMEM((864, 128), F32)
    trace = pltpu.VMEM((144, 128), F32)
    out = jax.ShapeDtypeStruct((576, 128), F32)

    def body(*refs):
        kernel(n_dom, n_sub, *refs)

    args = (coarse.reshape(576, 128), fine.reshape(576, 128), cel, cden, fel, fden, clinks, flinks, csend, fret,
            selem, samp.T, sshape.T, jnp.asarray(derivative_tables()))
    c, f = pl.pallas_call(
        body,
        name="lts",
        out_shape=(pltpu.VMEM((576, 128), F32), pltpu.VMEM((576, 128), F32)),
        in_specs=[hbm] * 14,
        out_specs=(vmem, vmem),
        scratch_shapes=[pltpu.VMEM(a.shape, a.dtype) for a in args]
        + [field] * 4
        + [faces] * 5
        + [trace] * 3
        + [pltpu.VMEM((3, 2, 72, 128), F32)] * 2
        + [pltpu.VMEM((3, 8, 24, 128), F32)] * 2
        + [pltpu.SemaphoreType.DMA((14,))]
        + [pltpu.SemaphoreType.DMA((3,))] * 4,
        compiler_params=pltpu.CompilerParams(collective_id=0, has_side_effects=True),
    )(*args)
    c, f = pl.pallas_call(
        store,
        name="put",
        out_shape=(out, out),
        in_specs=[vmem, vmem],
        out_specs=(hbm, hbm),
        scratch_shapes=[pltpu.SemaphoreType.DMA((2,))],
    )(pltpu.with_memory_space_constraint(c, pltpu.VMEM), pltpu.with_memory_space_constraint(f, pltpu.VMEM))
    return c.reshape(9, 64, 128), f.reshape(9, 64, 128)

def solution(mesh):
    n_dom, n_sub = mesh.shape["dom"], mesh.shape["sub"]
    every = ("dom", "sub")

    def body(*args):
        return per_device(n_dom, n_sub, *args)

    return jax.shard_map(
        body,
        mesh=mesh,
        in_specs=(
            P(None, None, every), P(None, None, every), P(None, every), P(every), P(None, every), P(every),
            P(None, every), P(None, every), P(every), P(every), P(every), P(None, every), P(None, every),
        ),
        out_specs=(P(None, None, every), P(None, None, every)),
        check_vma=False,
    )
```

```python
import math

import jax
import jax.numpy as jnp
import numpy as np
from jax import lax
from jax.experimental import pallas as pl
from jax.experimental.pallas import tpu as pltpu
from jax.sharding import PartitionSpec as P

MESH = pl.DeviceIdType.MESH
COARSE_DT = 0.03
FINE_DT = 0.015
ORDER = (4, 3, 5, 2, 6, 1, 7)
F32 = jnp.float32
BF16 = jnp.bfloat16


def derivative():
    points = np.array([-1.0, -1.0 / math.sqrt(5.0), 1.0 / math.sqrt(5.0), 1.0])
    bary = np.array([1.0 / np.prod([points[c] - points[o] for o in range(4) if o != c]) for c in range(4)])
    d = np.zeros((4, 4))
    for r in range(4):
        for c in range(4):
            if r != c:
                d[r, c] = bary[c] / bary[r] / (points[r] - points[c])
        d[r, r] = -np.sum(d[r])
    return d


def derivative_tables():
    d, eye = derivative(), np.eye(4)
    along_y = np.kron(np.kron(eye, d), eye)
    along_z = np.kron(np.eye(16), d)
    full = np.concatenate([along_y, along_z]).astype(np.float32)
    high = full.astype(BF16)
    low = (full - high.astype(np.float32)).astype(BF16)
    return np.concatenate([high, low, high], axis=1)


def kernel(n_dom, n_sub, *refs):
    hbm_refs, (out_c, out_f), vmem_refs = refs[:14], refs[14:16], refs[16:30]
    (qc, qf, cel, cden, fel, fden, clinks, flinks, csend, fret, selem, samp, sshape, dmat) = vmem_refs
    (ic, if_, c0, base_f, tc, t0, tf, jc, jf, tab_h, tab_i, ret0,
     hs, hr, xs, xr, in_sem, hs_sem, hr_sem, xs_sem, xr_sem) = refs[30:]

    dom, sub = lax.axis_index("dom"), lax.axis_index("sub")
    n_all = n_dom * n_sub
    here = dom * n_sub + sub
    above, below = lax.rem(here + 1, n_all), lax.rem(here + n_all - 1, n_all)
    above_id = (above // n_sub, lax.rem(above, n_sub))
    below_id = (below // n_sub, lax.rem(below, n_sub))

    barrier = pltpu.get_barrier_semaphore()
    for peer in (below_id, above_id):
        pl.semaphore_signal(barrier, inc=1, device_id=peer, device_id_type=MESH)
    for d in ORDER:
        pl.semaphore_signal(barrier, inc=1, device_id=(dom, lax.rem(sub + d, n_sub)), device_id_type=MESH)

    loads = [pltpu.make_async_copy(src, dst, in_sem.at[i]) for i, (src, dst) in enumerate(zip(hbm_refs, vmem_refs))]
    early = (1, 0, 4, 5, 2, 3, 13)
    late = (8, 7, 9, 6, 10, 11, 12)
    for i in early:
        loads[i].start()
    for i in late:
        loads[i].start()

    lane = lax.broadcasted_iota(jnp.int32, (1, 128), 1)
    lane_lo = lane < 64
    sub_lo = lax.broadcasted_iota(jnp.int32, (8, 1), 0) < 4

    def material(el, den, g):
        lame, shear = el[0:1, :], el[1:2, :]
        buoy = 1.0 / den[...].reshape(1, 128)
        speed = jnp.sqrt((lame + 2.0 * shear) * buoy)
        return lame * g, shear * g, buoy * g, speed * g


    table = derivative()

    def along_x(x):
        part = [x[16 * i : 16 * i + 16, :] for i in range(4)]
        out = []
        for i in range(4):
            terms = [float(table[i, k]) * part[k] for k in range(4) if abs(table[i, k]) > 1e-9]
            while len(terms) > 1:
                terms = [terms[n] + terms[n + 1] if n + 1 < len(terms) else terms[n] for n in range(0, len(terms), 2)]
            out.append(terms[0])
        return jnp.concatenate(out, axis=0)

    def split(x):
        high = x.astype(BF16)
        low = (x - high.astype(F32)).astype(BF16)
        return jnp.concatenate([high, high, low], axis=0)

    def along(pair, first, last):
        both = jnp.concatenate([split(x) for x in pair], axis=1)
        got = jnp.dot(dmat[64 * first : 64 * last, :], both, preferred_element_type=F32)
        return [[got[64 * i : 64 * i + 64, 128 * k : 128 * k + 128] for i in range(last - first)] for k in range(2)]

    def rates(src, mat, emit):
        lame, shear, buoy, _ = mat
        x = [src[64 * v : 64 * v + 64, :] for v in range(9)]
        (y6, z6), (y7, z7) = along((x[6], x[7]), 0, 2)
        (y8, z8), (y4, z4) = along((x[8], x[4]), 0, 2)
        (y3,), (y1,) = along((x[3], x[1]), 0, 1)
        (z5,), (z2,) = along((x[5], x[2]), 1, 2)
        x6, x7, x8, x0, x3, x5 = [along_x(x[v]) for v in (6, 7, 8, 0, 3, 5)]
        spread = lame * (x6 + y7 + z8)
        shear2 = 2.0 * shear
        out = [spread + shear2 * x6, spread + shear2 * y7, spread + shear2 * z8,
               shear * (y6 + x7), shear * (z7 + y8), shear * (z6 + x8),
               buoy * (x0 + y3 + z5), buoy * (x3 + y1 + z4), buoy * (x5 + y4 + z2)]
        for v in range(9):
            emit(v, out[v])

    def nested(dt, jobs):
        for src, _, out in jobs:
            out[...] = src[...]

        def order(k, _):
            outer = jnp.where(k == 2, dt, 1.0).astype(F32)
            inner = jnp.where(k == 0, dt / 4.0, jnp.where(k == 1, dt / 3.0, dt * dt / 2.0)).astype(F32)
            for src, mat, out in jobs:

                def emit(v, value, src=src, out=out):
                    at = slice(64 * v, 64 * v + 64)
                    out[at, :] = outer * src[at, :] + value

                rates(out, tuple(inner * m for m in mat), emit)
            return 0

        lax.fori_loop(0, 3, order, 0)

    def traces(src, out):
        for v in range(9):
            out[16 * v : 16 * v + 16, :] = src[64 * v : 64 * v + 16, :]
            out[144 + 16 * v : 160 + 16 * v, :] = src[64 * v + 48 : 64 * v + 64, :]
        blocks = src[...].reshape(18, 2, 16, 128)
        even, odd = blocks[:, 0, 0:8], blocks[:, 1, 0:8]
        out[288:432, :] = jnp.where(sub_lo[None], even, pltpu.roll(odd, 4, 1)).reshape(144, 128)
        even, odd = blocks[:, 0, 8:16], blocks[:, 1, 8:16]
        out[432:576, :] = jnp.where(sub_lo[None], pltpu.roll(even, 4, 1), odd).reshape(144, 128)
        out[576:720, :] = src[pl.ds(0, 144, stride=4), :]
        out[720:864, :] = src[pl.ds(3, 144, stride=4), :]

    def gather(table, index):
        return jnp.take_along_axis(table, jnp.broadcast_to(index, table.shape), axis=1, mode="promise_in_bounds")

    def face(ref, f):
        return ref[144 * f : 144 * f + 144, :]

    def face_columns(ref, columns):
        index, which = columns & 127, columns >> 7
        total = gather(face(ref, 0), index)
        for f in range(1, 6):
            total = jnp.where(which == f, gather(face(ref, f), index), total)
        return total

    block = lane >> 4

    def butterfly(parts):
        for step in (1, 2, 4):
            keep = (block & step) == 0
            fresh = list(parts)
            for i in range(8):
                if not i & step:
                    low, high = parts[i], parts[i + step]
                    fresh[i] = jnp.where(keep, low, pltpu.roll(high, 16 * step, 1))
                    fresh[i + step] = jnp.where(keep, pltpu.roll(low, 128 - 16 * step, 1), high)
            parts = fresh
        return parts

    def exchange_copy(phase, d):
        peer = lax.rem(sub + d, n_sub)
        return pltpu.make_async_remote_copy(
            src_ref=xs.at[phase, peer], dst_ref=xr.at[phase, sub],
            send_sem=xs_sem.at[0], recv_sem=xr_sem.at[phase],
            device_id=(dom, peer), device_id_type=MESH)

    def exchange_start(phase, value):
        exchange_pack(phase, value)
        exchange_send(phase)

    def exchange_pack(phase, value):
        parts = [value[24 * i : 24 * i + 24, :] for i in range(6)]
        parts = butterfly(parts + [parts[0], parts[0]])
        for b in range(8):
            xs[phase, b] = parts[b]

    def exchange_send(phase):
        for d in ORDER:
            exchange_copy(phase, d).start()

    def exchange_all(phase):
        return pltpu.make_async_remote_copy(
            src_ref=xs.at[phase, pl.ds(0, n_sub - 1)], dst_ref=xr.at[phase, pl.ds(0, n_sub - 1)],
            send_sem=xs_sem.at[0], recv_sem=xr_sem.at[phase],
            device_id=(dom, lax.rem(sub + 1, n_sub)), device_id_type=MESH)

    def exchange_wait(phase):
        exchange_all(phase).wait_recv()

    def exchange_read(phase):
        xr[phase, sub] = xs[phase, sub]
        parts = butterfly([xr[phase, a] for a in range(8)])
        return jnp.concatenate(parts[:6], axis=0)

    def halo_copies(phase):
        return [
            pltpu.make_async_remote_copy(
                src_ref=hs.at[phase, way], dst_ref=hr.at[phase, way],
                send_sem=hs_sem.at[0], recv_sem=hr_sem.at[phase],
                device_id=peer, device_id_type=MESH)
            for way, peer in enumerate((above_id, below_id))]

    def halo_pack(phase, ref):
        low, high = ref[720:792, :], ref[792:864, :]
        hs[phase, 0] = jnp.where(lane_lo, pltpu.roll(low, 64, 1), high)
        low, high = ref[576:648, :], ref[648:720, :]
        hs[phase, 1] = jnp.where(lane_lo, low, pltpu.roll(high, 64, 1))

    def halo_start(phase):
        for copy in halo_copies(phase):
            copy.start()

    def halo_all(phase):
        return pltpu.make_async_remote_copy(
            src_ref=hs.at[phase], dst_ref=hr.at[phase], send_sem=hs_sem.at[0], recv_sem=hr_sem.at[phase],
            device_id=above_id, device_id_type=MESH)

    def halo_wait(phase):
        halo_all(phase).wait_recv()

    def halo_read(phase):
        lower, upper = hr[phase, 0], hr[phase, 1]
        tab_h[0:72, :] = jnp.where(lane_lo, lower, pltpu.roll(upper, 64, 1))
        tab_h[72:144, :] = jnp.where(lane_lo, pltpu.roll(lower, 64, 1), upper)

    def pick(links, f, table, low):
        row = links[f : f + 1, :]
        hit = (row >= low) & (row < low + 128)
        return jnp.where(hit, gather(table, row & 127), 0.0)

    def jump_own(links, t, j):
        for f in range(6):
            j[144 * f : 144 * f + 144, :] = pick(links, f, face(t, f ^ 1), 0) - face(t, f)

    def jump_add(links, j, table, low):
        for f in range(6):
            j[144 * f : 144 * f + 144, :] = face(j, f) + pick(links, f, table[...], low)

    def lift(mat, j, base, extra):
        lame, shear, buoy, speed = [3.0 * m for m in mat]
        full = lame + 2.0 * shear
        normal = (6, 7, 8)
        stress = ((0, 3, 5), (3, 1, 4), (5, 4, 2))
        for f in range(6):
            axis, sign = f // 2, 1.0 if f % 2 else -1.0
            jump = face(j, f)
            if len(extra) == 1:
                (links, table_ref, low), = extra
                jump = jump + pick(links, f, table_ref[...], low)
            else:
                row = flinks[f : f + 1, :]
                index = row & 127
                outer = jnp.where(row < 256, gather(tab_h[...], index), gather(tab_i[...], index))
                jump = jump + jnp.where(row < 128, 0.0, outer)
            part = [jump[16 * v : 16 * v + 16, :] for v in range(9)]
            vel = part[normal[axis]]
            lam_s, full_s, shear_s, buoy_s = sign * lame, sign * full, sign * shear, sign * buoy
            out = [None] * 9
            for v in range(3):
                out[v] = speed * part[v] + (full_s if v == axis else lam_s) * vel
            pairs = {3: (0, 1), 4: (1, 2), 5: (0, 2)}
            for v, (a, b) in pairs.items():
                out[v] = speed * part[v]
                if axis in (a, b):
                    out[v] = out[v] + shear_s * part[6 + (b if axis == a else a)]
            for v in range(3):
                out[6 + v] = speed * part[6 + v] + buoy_s * part[stress[axis][v]]
            if axis == 0:
                for v in range(9):
                    at = slice(64 * v + 48 * (f % 2), 64 * v + 48 * (f % 2) + 16)
                    base[at, :] = base[at, :] + out[v]
            elif axis == 1:
                for v in range(9):
                    for p in range(2):
                        c = out[v][8 * p : 8 * p + 8, :]
                        r = pltpu.roll(c, 4, 0)
                        at = 64 * v + 32 * p + 8 * (f % 2)
                        if f % 2:
                            first, second = jnp.where(sub_lo, 0.0, r), jnp.where(sub_lo, 0.0, c)
                        else:
                            first, second = jnp.where(sub_lo, c, 0.0), jnp.where(sub_lo, r, 0.0)
                        base[at : at + 8, :] = base[at : at + 8, :] + first
                        base[at + 16 : at + 24, :] = base[at + 16 : at + 24, :] + second
            else:
                for v in range(9):
                    at = pl.ds(64 * v + 3 * (f % 2), 16, stride=4)
                    base[at, :] = base[at, :] + out[v]

    def start_base(q, integral, mat, base):
        def emit(v, value):
            at = slice(64 * v, 64 * v + 64)
            base[at, :] = q[at, :] + value

        rates(integral, mat, emit)


    for i in early:
        loads[i].wait()
    mat_f = material(fel, fden, 2.0)
    mat_c = material(cel, cden, 1.0)
    nested(FINE_DT, ((qf, mat_f, if_), (qc, mat_c, c0)))
    traces(if_, tf)
    halo_pack(0, tf)
    for i in late:
        loads[i].wait()
    send_row = csend[...].reshape(1, 128)
    return_row = fret[...].reshape(1, 128)
    traces(c0, t0)
    first = face_columns(t0, send_row)
    exchange_pack(0, first)
    pl.semaphore_wait(barrier, n_sub + 1)
    halo_start(0)
    exchange_send(0)

    nested(COARSE_DT, ((qc, mat_c, ic),))
    traces(ic, tc)
    second = face_columns(tc, send_row) - first
    halo_pack(1, tc)
    exchange_start(1, second)
    halo_start(1)
    start_base(qf, if_, mat_f, base_f)
    jump_own(flinks, tf, jf)
    ret0[...] = face_columns(tf, return_row)

    halo_wait(0)
    halo_read(0)
    jump_add(flinks, jf, tab_h, 128)
    exchange_wait(0)
    tab_i[...] = exchange_read(0)
    lift(mat_f, jf, base_f, ((flinks, tab_i, 256),))
    nested(FINE_DT, ((base_f, mat_f, if_),))
    traces(if_, tf)
    halo_pack(2, tf)
    halo_start(2)
    exchange_start(2, ret0[...] + face_columns(tf, return_row))

    start_base(base_f, if_, mat_f, out_f)
    jump_own(flinks, tf, jf)
    start_base(qc, ic, mat_c, out_c)
    jump_own(clinks, tc, jc)
    node_of, amp = sshape[...], COARSE_DT * samp[...]
    square = lax.broadcasted_iota(jnp.int32, (4, 4), 0) == lax.broadcasted_iota(jnp.int32, (4, 4), 1)
    spot = selem[...].astype(F32).reshape(1, 4)
    column = jnp.sum(jnp.where(square, spot, 0.0), axis=1, keepdims=True)
    hit = lane.astype(F32) == column
    for v in range(9):
        field = lax.dot_general(node_of, jnp.where(hit, amp[:, v : v + 1], 0.0), (((0,), (0,)), ((), ())),
                                precision=lax.Precision.HIGHEST, preferred_element_type=F32)
        out_c[64 * v : 64 * v + 64, :] = out_c[64 * v : 64 * v + 64, :] + field
    exchange_wait(1)
    tab_i[...] = exchange_read(1)
    jump_add(flinks, jf, tab_i, 256)
    halo_wait(1)
    halo_read(1)
    jump_add(clinks, jc, tab_h, 128)

    pltpu.make_async_remote_copy(
        src_ref=hs, dst_ref=hr, send_sem=hs_sem.at[0], recv_sem=hr_sem.at[0],
        device_id=above_id, device_id_type=MESH).wait_send()
    part = pl.ds(0, n_sub - 1)
    pltpu.make_async_remote_copy(
        src_ref=xs.at[pl.ds(0, 3), part], dst_ref=xr.at[pl.ds(0, 3), part], send_sem=xs_sem.at[0], recv_sem=xr_sem.at[0],
        device_id=above_id, device_id_type=MESH).wait_send()
    halo_wait(2)
    halo_read(2)
    lift(mat_f, jf, out_f, ((flinks, tab_h, 128),))
    exchange_wait(2)
    tab_i[...] = exchange_read(2)
    lift(mat_c, jc, out_c, ((clinks, tab_i, 256),))


def store(c_ref, f_ref, outc_ref, outf_ref, sem):
    copies = [pltpu.make_async_copy(src, dst, sem.at[i]) for i, (src, dst) in enumerate(((c_ref, outc_ref), (f_ref, outf_ref)))]
    for piece in copies:
        piece.start()
    for piece in copies:
        piece.wait()


def per_device(n_dom, n_sub, coarse, fine, cel, cden, fel, fden, clinks, flinks, csend, fret, selem, samp, sshape):
    hbm = pl.BlockSpec(memory_space=pl.ANY)
    vmem = pl.BlockSpec(memory_space=pltpu.VMEM)
    field = pltpu.VMEM((576, 128), F32)
    faces = pltpu.VMEM((864, 128), F32)
    trace = pltpu.VMEM((144, 128), F32)
    out = jax.ShapeDtypeStruct((576, 128), F32)

    def body(*refs):
        kernel(n_dom, n_sub, *refs)

    args = (coarse.reshape(576, 128), fine.reshape(576, 128), cel, cden, fel, fden, clinks, flinks, csend, fret,
            selem, samp.T, sshape.T, jnp.asarray(derivative_tables()))
    c, f = pl.pallas_call(
        body,
        name="lts",
        out_shape=(pltpu.VMEM((576, 128), F32), pltpu.VMEM((576, 128), F32)),
        in_specs=[hbm] * 14,
        out_specs=(vmem, vmem),
        scratch_shapes=[pltpu.VMEM(a.shape, a.dtype) for a in args]
        + [field] * 4
        + [faces] * 5
        + [trace] * 3
        + [pltpu.VMEM((3, 2, 72, 128), F32)] * 2
        + [pltpu.VMEM((3, 8, 24, 128), F32)] * 2
        + [pltpu.SemaphoreType.DMA((14,))]
        + [pltpu.SemaphoreType.DMA((1,)), pltpu.SemaphoreType.DMA((3,))] * 2,
        compiler_params=pltpu.CompilerParams(collective_id=0, has_side_effects=True),
    )(*args)
    c, f = pl.pallas_call(
        store,
        name="put",
        out_shape=(out, out),
        in_specs=[vmem, vmem],
        out_specs=(hbm, hbm),
        scratch_shapes=[pltpu.SemaphoreType.DMA((2,))],
    )(pltpu.with_memory_space_constraint(c, pltpu.VMEM), pltpu.with_memory_space_constraint(f, pltpu.VMEM))
    return c.reshape(9, 64, 128), f.reshape(9, 64, 128)


def solution(mesh):
    n_dom, n_sub = mesh.shape["dom"], mesh.shape["sub"]
    every = ("dom", "sub")

    def body(*args):
        return per_device(n_dom, n_sub, *args)

    return jax.shard_map(
        body,
        mesh=mesh,
        in_specs=(
            P(None, None, every), P(None, None, every), P(None, every), P(every), P(None, every), P(every),
            P(None, every), P(None, every), P(every), P(every), P(every), P(None, every), P(None, every),
        ),
        out_specs=(P(None, None, every), P(None, None, every)),
        check_vma=False,
    )
```
